128 devices in a mesh: dp: 8 (over z, core), fsdp: 16 (over x, y).
Axes of the slice: x: 4, y: 4, z: 4, core: 2. Of those that a mesh axis runs over, the one named last changes fastest.
Arguments:
- gate_act: bfloat16 [4096, 14848], P('fsdp', 'dp'), may hold values from -6 to 6
- up_act: bfloat16 [4096, 14848], P('fsdp', 'dp'), may hold values from -6 to 6
- out_grad: bfloat16 [4096, 4096], P('fsdp'), may hold values from -6 to 6
- master_old: float32 [8, 2176, 4096], P('dp', 'fsdp'), may hold values from -0.046875 to 0.046875
- moment1_old: float32 [8, 2176, 4096], P('dp', 'fsdp'), may hold values from -4 to 4
- moment2_old: float32 [8, 2176, 4096], P('dp', 'fsdp'), may hold values from 0.02 to 4
- old_bounds: int32 [8, 17], P('dp'), may hold values from 0 to 1856, as said below
- new_bounds: int32 [8, 16], P('dp'), may hold values from 0 to 1856, as said below
- rank_map: int32 [8, 16], P('dp'), may hold values from 0 to 15, as said below
Outputs:
- mlp_out: float32 [4096, 4096], P('fsdp', 'dp')
- master_new: float32 [8, 2176, 4096], P('dp', 'fsdp')
- moment1_new: float32 [8, 2176, 4096], P('dp', 'fsdp')
- moment2_new: float32 [8, 2176, 4096], P('dp', 'fsdp')
The draws below stay inside these ranges and needn't reach their ends.
Inputs may be any that keep to these rules, and one draw needn't show every extreme that they name: Each row of old_bounds starts at 0, ends at 1856 and never falls; each position's rows fit its 136 slots. Each row of new_bounds starts at 0, ends at 1856 and never falls; each rank's rows fit 136 slots. In every block a position's new rows lie within its old rows and at most 58 rows of each of its two neighbours. `rank_map`: in each block's row exactly one position, one of the two middle ones, has rank 16 - 1 and owns nothing; the others hold the ranks 0 to 14 in position order.
All inputs are finite; a program needn't handle non-finite values.
Results may differ from the reference program's by a relative error of at most 0.012.
Values may be sent and summed in bfloat16 or wider, within the bound.
A program may use at most 192 MiB of HBM per device.

```python
import math
import jax
import jax.numpy as jnp
from jax import lax

D = 4096
FF = 14848
TOK_DEV = 256
TOKENS = 4096
HID = 1856
CAP = 136
N_DP = 8
N_FSDP = 16


def block_layout(key, block):
    ranks_total = N_FSDP
    block_rows = FF // N_DP
    base_rows = block_rows // ranks_total
    key_bump, key_lost, key_edge = jax.random.split(jax.random.fold_in(key, 100 + block), 3)
    lost_slot = ranks_total // 2 - 1 + jax.random.randint(key_lost, (), 0, 2)
    rank_index = jnp.arange(ranks_total)
    bump_values = jax.random.randint(key_bump, (ranks_total,), 0, 2)
    bump_values = jnp.where(rank_index == lost_slot, jnp.roll(bump_values, 1), bump_values)
    row_counts = base_rows + bump_values - jnp.roll(bump_values, 1)
    old_bounds = jnp.concatenate([jnp.zeros((1,), jnp.int32), jnp.cumsum(row_counts).astype(jnp.int32)])
    left_share = base_rows // 2
    right_share = base_rows - left_share
    position = jnp.arange(ranks_total + 1)
    left_shift = left_share * position // lost_slot
    right_shift = -(right_share * (ranks_total - position) // (ranks_total - 1 - lost_slot))
    shift = jnp.where(position <= lost_slot, left_shift, right_shift)
    edge = jax.random.randint(key_edge, (2,), 1, 3)
    sign = 1 if block % 2 == 0 else -1
    shift = jnp.where(position == 1, sign * edge[0], shift)
    shift = jnp.where(position == ranks_total - 1, sign * edge[1], shift)
    boundary = old_bounds + shift
    new_bounds = jnp.where(rank_index < lost_slot, boundary[:ranks_total], boundary[1:])
    rank_map = jnp.where(rank_index < lost_slot, rank_index, jnp.where(rank_index == lost_slot, ranks_total - 1, rank_index - 1))
    return (old_bounds.astype(jnp.int32), new_bounds.astype(jnp.int32), rank_map.astype(jnp.int32))


def layout_ints(key):
    pieces = [block_layout(key, block) for block in range(N_DP)]
    return tuple((jnp.stack([piece[index] for piece in pieces]) for index in range(3)))


def draw_old_bounds(key, part):
    return layout_ints(key)[0]


def draw_new_bounds(key, part):
    return layout_ints(key)[1]


def draw_rank_map(key, part):
    return layout_ints(key)[2]


def block_levels(key, dims, cuts, least, high):
    factor_of = 1.0
    for dim, parts in cuts:
        steps = jax.random.uniform(jax.random.fold_in(jax.random.fold_in(key, 6), dim), (parts,), jnp.float32, least / len(cuts), high / len(cuts))
        factor_of = factor_of * jnp.repeat(jnp.exp(steps), dims[dim] // parts).reshape((-1,) + (1,) * (len(dims) - 1 - dim))
    return factor_of


def centred(own_key, extent, deviation, limit, cuts=(), kind=jnp.bfloat16):
    array = jax.random.normal(own_key, extent, jnp.float32) * deviation
    if len(cuts) > 0:
        array = block_levels(own_key, extent, cuts, -0.22, 0.18) * array
    return jnp.clip(array, min=-limit, max=limit).astype(kind)


def setup_inputs(seed: int = 0) -> dict:
    key_of = jax.random.split(jax.random.key(seed), 10)
    gate_act = centred(key_of[0], (TOKENS, FF), 1.0, 6.0, ((0, 16), (1, 8)))
    up_act = centred(key_of[1], (TOKENS, FF), 1.0, 6.0, ((0, 16), (1, 8)))
    out_grad = centred(key_of[2], (TOKENS, D), 1.0, 6.0, ((0, 16),))
    master_old = centred(key_of[3], (N_DP, N_FSDP * CAP, D), FF ** -0.5, 0.046875, ((0, 8), (1, 16)), jnp.float32)
    moment1_old = centred(key_of[4], (N_DP, N_FSDP * CAP, D), 0.6, 4.0, ((0, 8), (1, 16)), jnp.float32)
    moment2_old = jnp.clip(jnp.exp(math.log(4.0) - 5.2983174 * jax.random.uniform(key_of[5], (N_DP, N_FSDP * CAP, D), jnp.float32) ** block_levels(key_of[5], (N_DP, N_FSDP * CAP, D), ((0, 8), (1, 16)), -0.2, 0.2)), 0.02, 4.0)
    old_bounds = draw_old_bounds(jax.random.fold_in(key_of[9], 71), 0)
    new_bounds = draw_new_bounds(jax.random.fold_in(key_of[9], 71), 0)
    rank_map = draw_rank_map(jax.random.fold_in(key_of[9], 71), 0)
    return dict(gate_act=gate_act, up_act=up_act, out_grad=out_grad, master_old=master_old, moment1_old=moment1_old, moment2_old=moment2_old, old_bounds=old_bounds, new_bounds=new_bounds, rank_map=rank_map)


def reference(gate_act, up_act, out_grad, master_old, moment1_old, moment2_old, old_bounds, new_bounds, rank_map):
    rows = jnp.arange(HID, dtype=jnp.int32)
    masters = []
    firsts = []
    seconds = []
    for block in range(N_DP):
        bounds = old_bounds[block]
        owner = lax.optimization_barrier(jnp.sum((bounds[1:][None, :] <= rows[:, None]).astype(jnp.int32), axis=1)).astype(jnp.int32)
        slot = (owner * CAP + rows - bounds[owner]).astype(jnp.int32)
        masters.append(jnp.take(master_old[block], slot, axis=0))
        firsts.append(jnp.take(moment1_old[block], slot, axis=0))
        seconds.append(jnp.take(moment2_old[block], slot, axis=0))
    weight_master = jnp.stack(masters)
    moment_first = jnp.stack(firsts)
    moment_second = jnp.stack(seconds)
    weight_low = weight_master.astype(jnp.bfloat16)
    hidden = (jax.nn.silu(gate_act.astype(jnp.float32)) * up_act.astype(jnp.float32)).astype(jnp.bfloat16)
    total = jnp.zeros((TOKENS, D), jnp.float32)
    for block in range(N_DP):
        part = jnp.dot(hidden[:, block * HID:(block + 1) * HID], weight_low[block], preferred_element_type=jnp.float32)
        rounded = lax.optimization_barrier(part.astype(jnp.bfloat16))
        total = total + rounded.astype(jnp.float32)
    mlp_out = total
    grouped_hidden = hidden.reshape(N_FSDP, TOK_DEV, FF)
    grouped_grad = out_grad.reshape(N_FSDP, TOK_DEV, D)

    def accumulate(carry, pair):
        hidden_part, grad_part = pair
        term = jnp.dot(hidden_part.T, grad_part, preferred_element_type=jnp.float32).astype(jnp.bfloat16)
        return (carry + term.astype(jnp.float32), None)
    summed, _ = lax.scan(accumulate, jnp.zeros((FF, D), jnp.float32), (grouped_hidden, grouped_grad))
    grad = (summed * (1.0 / math.sqrt(TOKENS))).reshape(N_DP, HID, D)
    first_next = 0.9 * moment_first + 0.1 * grad
    second_next = 0.95 * moment_second + 0.05 * grad * grad
    master_next = weight_master - 0.001 * (first_next / (jnp.sqrt(second_next) + 1e-08) + 0.1 * weight_master)
    slots = jnp.arange(N_FSDP * CAP, dtype=jnp.int32)
    position = slots // CAP
    within = slots % CAP
    out_master = []
    out_first = []
    out_second = []
    for block in range(N_DP):
        new_rank = rank_map[block][position]
        extended = jnp.concatenate([new_bounds[block], new_bounds[block][-1:]])
        start_row = extended[new_rank]
        live_rows = extended[new_rank + 1] - start_row
        valid = within < live_rows
        source = jnp.clip(start_row + within, 0, HID - 1).astype(jnp.int32)

        def placed(values):
            chosen = jnp.take(values, source, axis=0)
            return jnp.where(valid[:, None], chosen, jnp.zeros_like(chosen))
        out_master.append(placed(master_next[block]))
        out_first.append(placed(first_next[block]))
        out_second.append(placed(second_next[block]))
    return (mlp_out, jnp.stack(out_master), jnp.stack(out_first), jnp.stack(out_second))
```

```python
import functools
import math

import jax
import jax.numpy as jnp
from jax import lax
from jax.experimental import pallas as pl
from jax.experimental.pallas import tpu as pltpu
from jax.sharding import PartitionSpec as P

BF = jnp.bfloat16
F32 = jnp.float32
MESH = pl.DeviceIdType.MESH

SIDE = 4
POS = 16
CAP = 136
PITCH = 144
HID = 1856
HIDP = 1920
D = 4096
COLS = D // SIDE
TOK = 256
EDGE = 64
SLACK = 320
HALF = 2 * PITCH
SLOTS = POS * PITCH
OFFS = (0, 1, 3, 2)


def window(first, size):
    low, high = HIDP, 0
    for p in range(POS):
        r0 = max(0, first - p * PITCH)
        r1 = min(CAP, first + size - p * PITCH)
        if r0 < r1:
            low = min(low, max(0, CAP * p - SLACK) + r0)
            high = max(high, min(HID, CAP * p) + r1)
    high = min(high, HID)
    low = low // 128 * 128
    high = -(-high // 128) * 128
    return low, high - low


NEW_WIN = [window(HALF * b, HALF) for b in range(8)]
OLD_WIN = [window(256 * b, 256) for b in range(SLOTS // 256)]
NEW_MAX = max(w for _, w in NEW_WIN)
OLD_MAX = max(w for _, w in OLD_WIN)


def prep_kernel(ob, nb, rm, gate, up, master, first, second, tab, hid, wq, pre, suf, buf):
    step = pl.program_id(0)
    me = lax.axis_index("fsdp")

    @pl.when(step == 0)
    def _():
        for p in range(POS):
            tab[0, p] = ob[0, p]
            tab[1, p] = ob[0, p + 1] - ob[0, p]
            k = rm[0, p]
            start = nb[0, k]
            tab[2, p] = start
            tab[3, p] = nb[0, jnp.minimum(k + 1, POS - 1)] - start
        buf[:, pl.ds(0, EDGE), :] = jnp.zeros((buf.shape[0], EDGE, 128), F32)

    g = gate[...].astype(F32)
    h = (g * jax.nn.sigmoid(g) * up[...].astype(F32)).astype(BF)
    hid[:, pl.ds(0, HID)] = h
    hid[:, pl.ds(HID, HIDP - HID)] = jnp.zeros((h.shape[0], HIDP - HID), BF)

    count = ob[0, me + 1] - ob[0, me]
    wq[0, pl.ds(0, CAP), :] = master[0].astype(BF)
    wq[0, pl.ds(CAP, PITCH - CAP), :] = jnp.zeros((PITCH - CAP, COLS), BF)
    for a, ref in enumerate((master, first, second)):
        pre[a] = ref[0, pl.ds(0, EDGE), :].astype(BF)
        for j in range(COLS // 128):
            lanes = pl.ds(128 * j, 128)
            buf[j, pl.ds(EDGE, CAP), :] = ref[0, :, lanes]
            suf[a, :, lanes] = buf[j, pl.ds(count, EDGE), :].astype(BF)


def prep(ob, nb, rm, gate, up, master, first, second):
    state = pl.BlockSpec((1, CAP, COLS), lambda i: (0, 0, i))
    act = pl.BlockSpec((TOK // 4, HID), lambda i: (i, 0))
    smem = pl.BlockSpec(memory_space=pltpu.SMEM)
    edge = pl.BlockSpec((3, EDGE, COLS), lambda i: (0, 0, i))
    return pl.pallas_call(
        prep_kernel,
        grid=(4,),
        in_specs=[smem, smem, smem, act, act, state, state, state],
        out_specs=[
            smem,
            pl.BlockSpec((TOK // 4, HIDP), lambda i: (i, 0)),
            pl.BlockSpec((1, PITCH, COLS), lambda i: (i, 0, 0)),
            edge,
            edge,
        ],
        out_shape=[
            jax.ShapeDtypeStruct((4, POS), jnp.int32),
            jax.ShapeDtypeStruct((TOK, HIDP), BF),
            jax.ShapeDtypeStruct((SIDE, PITCH, COLS), BF),
            jax.ShapeDtypeStruct((3, EDGE, D), BF),
            jax.ShapeDtypeStruct((3, EDGE, D), BF),
        ],
        scratch_shapes=[pltpu.VMEM((COLS // 128, EDGE + CAP + EDGE, 128), F32)],
        name="prep",
    )(ob, nb, rm, gate, up, master, first, second)


def main_kernel(
    tab, hid, wq, og, pre, suf,
    mlp, grad, from_left, from_right,
    h_all, w_all, g_stage, g_all, s_new, s_old, hn, p_acc, part, ho,
    ra2, rb2, rad, rbd, rac, rbc, ca, cb, s_fin,
    c_part, c_sib, c_sum, c_y, c_z,
    send, recv, loc,
):
    dp = lax.axis_index("dp")
    f = lax.axis_index("fsdp")
    z, c = dp // 2, dp % 2
    x, y = f // SIDE, f % SIDE

    def dev(dx=0, dy=0, dz=0, dc=0):
        return (
            (z + dz) % SIDE * 2 + (c + dc) % 2,
            (x + dx) % SIDE * SIDE + (y + dy) % SIDE,
        )

    right = (dp, (f + 1) % POS)
    left = (dp, (f + POS - 1) % POS)
    peers = [dev(dy=d, dc=e) for d in (1, 2, 3) for e in (0, 1)]
    peers += [dev(dx=1), dev(dx=3)]
    peers += [dev(dz=d, dc=e) for d in range(SIDE) for e in (0, 1) if (d, e) != (0, 0)]
    peers += [right, left]

    counter = [0]
    sent = []

    def remote(src, dst, device):
        n = counter[0]
        counter[0] += 1
        copy = pltpu.make_async_remote_copy(
            src_ref=src,
            dst_ref=dst,
            send_sem=send.at[n],
            recv_sem=recv.at[n],
            device_id=device,
            device_id_type=MESH,
        )
        copy.start()
        sent.append(copy)
        return copy

    locals_used = [0]

    def local_copy(src, dst):
        n = locals_used[0]
        locals_used[0] += 1
        copy = pltpu.make_async_copy(src, dst, loc.at[n])
        copy.start()
        return copy

    barrier = pltpu.get_barrier_semaphore()
    for peer in peers:
        pl.semaphore_signal(barrier, inc=1, device_id=peer, device_id_type=MESH)
    pl.semaphore_wait(barrier, len(peers))

    def tok_rows(ref, k, n=1):
        return ref.at[pl.ds(k * TOK, n * TOK)]

    def w_slot(dx, dy):
        pos = (x + dx) % SIDE * SIDE + (y + dy) % SIDE
        return w_all.at[pl.ds(pl.multiple_of(pos * PITCH, PITCH), PITCH)]

    share = pl.multiple_of(dp * 32, 32)
    rel = {d: OFFS.index(d) for d in range(SIDE)}
    g_copies = {}
    for d in (1, 3, 2):
        cols = pl.multiple_of((y + d) % SIDE * COLS, COLS)
        g_copies[d] = remote(
            og.at[pl.ds(share, 32), pl.ds(cols, COLS)], g_stage.at[rel[(-d) % SIDE]], dev(dy=d)
        )
    g_own = local_copy(
        og.at[pl.ds(share, 32), pl.ds(pl.multiple_of(y * COLS, COLS), COLS)], g_stage.at[0]
    )
    w_y = {}
    for d in (1, 3, 2):
        w_y[d] = remote(wq.at[(y + d) % SIDE], w_slot(0, 0), dev(dy=d))
    w_own = local_copy(wq.at[y], w_slot(0, 0))
    wx_plus, wx_minus = {}, {}
    wx_plus[0] = remote(wq.at[y], w_slot(0, 0), dev(dx=1))
    wx_minus[0] = remote(wq.at[y], w_slot(0, 0), dev(dx=3))
    h_plus = remote(hid, tok_rows(h_all, rel[3]), dev(dy=1))
    h_minus = remote(hid, tok_rows(h_all, rel[1]), dev(dy=3))
    h_own = local_copy(hid, tok_rows(h_all, 0))

    for b, (low, wide) in enumerate(NEW_WIN):
        row = lax.broadcasted_iota(jnp.int32, (HALF, 1), 0)
        upper = row >= PITCH
        r = jnp.where(upper, row - PITCH, row)
        start = jnp.where(upper, tab[2, 2 * b + 1], tab[2, 2 * b])
        count = jnp.where(upper, tab[3, 2 * b + 1], tab[3, 2 * b])
        col = jnp.where(r < count, start + r - low, -1)
        lane = lax.broadcasted_iota(jnp.int32, (HALF, wide), 1)
        s_new[pl.ds(HALF * b, HALF), pl.ds(0, wide)] = jnp.where(lane == col, 1.0, 0.0).astype(BF)
    for b, (low, wide) in enumerate(OLD_WIN):
        slot = lax.broadcasted_iota(jnp.int32, (1, 256), 1) + 256 * b
        col = jnp.full((1, 256), -1, jnp.int32)
        for p in range(256 * b // PITCH, min(POS - 1, (256 * b + 255) // PITCH) + 1):
            r = slot - p * PITCH
            col = jnp.where((r >= 0) & (r < tab[1, p]), tab[0, p] + r - low, col)
        row = lax.broadcasted_iota(jnp.int32, (wide, 256), 0)
        s_old[pl.ds(0, wide), pl.ds(256 * b, 256)] = jnp.where(row == col, 1.0, 0.0).astype(BF)

    g_own.wait()
    for d in (1, 3, 2):
        g_copies[d].wait_recv()

    def g_slot(k):
        return g_all.at[pl.ds(k * TOK + share, 32)]

    g_out = []
    for e, d in ((1, 0), (0, 1), (0, 3), (1, 1), (1, 3), (0, 2), (1, 2)):
        g_out.append([remote(g_stage.at[k], g_slot(k), dev(dz=d, dc=e)) for k in range(SIDE)])
    g_loc = [local_copy(g_stage.at[k], g_slot(k)) for k in range(SIDE)]

    for d in (1, 3, 2):
        w_y[d].wait_recv()
        piece = w_slot(0, -d)
        wx_plus[d] = remote(piece, piece, dev(dx=1))
        wx_minus[d] = remote(piece, piece, dev(dx=3))
    w_far = []
    for d in (0, 1, 3, 2):
        wx_plus[d].wait_recv()
        wx_minus[d].wait_recv()
        if d in (0, 1):
            piece = w_slot(-1, -d)
            w_far.append(remote(piece, piece, dev(dx=1)))
        else:
            piece = w_slot(1, -d)
            w_far.append(remote(piece, piece, dev(dx=3)))

    h_plus.wait_recv()
    h_minus.wait_recv()
    h_far_plus = remote(
        h_all.at[pl.ds(rel[3] * TOK, 128)], h_all.at[pl.ds(rel[2] * TOK, 128)], dev(dy=1)
    )
    h_far_minus = remote(
        h_all.at[pl.ds(rel[1] * TOK + 128, 128)],
        h_all.at[pl.ds(rel[2] * TOK + 128, 128)],
        dev(dy=3),
    )
    m_right = remote(suf, from_left, right)
    m_left = remote(pre, from_right, left)

    h_own.wait()
    for k in range(SIDE):
        g_loc[k].wait()
    for group in g_out:
        for copy in group:
            copy.wait_recv()

    def grad_rows(b, first, count):
        low, wide = NEW_WIN[b]
        toks = pl.ds(first * TOK, count * TOK)
        rows = pl.ds(HALF * b, HALF)
        hn[:, pl.ds(0, count * TOK)] = lax.dot_general(
            s_new[rows, pl.ds(0, wide)],
            h_all[toks, pl.ds(low, wide)],
            (((1,), (1,)), ((), ())),
            preferred_element_type=F32,
        ).astype(BF)
        return jnp.dot(
            hn[:, pl.ds(0, count * TOK)], g_all[toks, :], preferred_element_type=F32
        )

    for b in range(8):
        p_acc[b] = grad_rows(b, 0, 3)
    h_far_plus.wait_recv()
    h_far_minus.wait_recv()
    for b in range(8):
        part[b] = (p_acc[b] + grad_rows(b, 3, 1)).astype(BF)

    def slab(dx, half):
        return part.at[(x + dx) % SIDE * 2 + half]

    copy_b2 = remote(slab(2, 1), rb2, dev(dx=1))
    copy_a2 = remote(slab(2, 0), ra2, dev(dx=3))
    copy_ad = remote(slab(1, 0), rad, dev(dx=1))
    copy_bd = remote(slab(3, 1), rbd, dev(dx=3))

    w_own.wait()
    for copy in w_far:
        copy.wait_recv()

    def forward(k):
        toks = pl.ds(pl.multiple_of(k * TOK, TOK), TOK)
        for b, (low, wide) in enumerate(OLD_WIN):
            ho[:, pl.ds(256 * b, 256)] = jnp.dot(
                h_all[toks, pl.ds(low, wide)],
                s_old[pl.ds(0, wide), pl.ds(256 * b, 256)],
                preferred_element_type=F32,
            ).astype(BF)
        c_part[k] = jnp.dot(ho[...], w_all[...], preferred_element_type=F32).astype(BF)

    @pl.loop(0, SIDE)
    def _(k):
        forward(k)

    theirs = pl.multiple_of((1 - c) * 128, 128)
    mine = pl.multiple_of(c * 128, 128)
    copy_sib = remote(c_part.at[:, pl.ds(theirs, 128)], c_sib, dev(dc=1))

    copy_b2.wait_recv()
    cb[...] = (rb2[...].astype(F32) + part[(x + 1) % SIDE * 2 + 1].astype(F32)).astype(BF)
    copy_bc = remote(cb, rbc, dev(dx=1))
    copy_a2.wait_recv()
    ca[...] = (ra2[...].astype(F32) + part[(x + 3) % SIDE * 2].astype(F32)).astype(BF)
    copy_ac = remote(ca, rac, dev(dx=3))

    copy_sib.wait_recv()
    c_sum[...] = (
        c_part[:, pl.ds(mine, 128), :].astype(F32) + c_sib[...].astype(F32)
    ).astype(BF)
    c_copies = []
    for d in (2, 1, 3, 0):
        for e in (0, 1):
            src = c_sum.at[rel[d], :, pl.ds(pl.multiple_of((c + e) % 2 * 512, 512), 512)]
            dst = c_y.at[y, pl.ds(mine, 128)]
            if (d, e) == (0, 0):
                c_own = local_copy(src, dst)
            else:
                c_copies.append(remote(src, dst, dev(dy=d, dc=e)))
    c_own.wait()
    for copy in c_copies:
        copy.wait_recv()
    z_copies = [remote(c_y.at[(z + d) % SIDE], c_z.at[d - 1], dev(dz=d)) for d in (2, 1, 3)]

    copy_ad.wait_recv()
    copy_ac.wait_recv()
    total = part[x * 2].astype(F32) + rad[...].astype(F32) + rac[...].astype(F32)
    s_fin[pl.ds(0, 2)] = total.astype(BF).reshape(2, PITCH, COLS)
    copy_bd.wait_recv()
    copy_bc.wait_recv()
    total = part[x * 2 + 1].astype(F32) + rbd[...].astype(F32) + rbc[...].astype(F32)
    s_fin[pl.ds(2, 2)] = total.astype(BF).reshape(2, PITCH, COLS)
    r_copies = [remote(s_fin.at[(y + d) % SIDE], grad.at[y], dev(dy=d)) for d in (2, 1, 3)]
    r_own = local_copy(s_fin.at[y], grad.at[y])

    for copy in z_copies:
        copy.wait_recv()
    mlp[...] = (
        c_y[z].astype(F32) + c_z[0].astype(F32) + c_z[1].astype(F32) + c_z[2].astype(F32)
    )
    r_own.wait()
    for copy in r_copies:
        copy.wait_recv()
    m_right.wait_recv()
    m_left.wait_recv()
    for copy in sent:
        copy.wait_send()


def exchange(tab, hid, wq, og, pre, suf):
    anywhere = pl.BlockSpec(memory_space=pl.ANY)
    vmem = pl.BlockSpec(memory_space=pltpu.VMEM)
    half = pltpu.VMEM((HALF, COLS), BF)
    return pl.pallas_call(
        main_kernel,
        in_specs=[pl.BlockSpec(memory_space=pltpu.SMEM)] + [anywhere] * 5,
        out_specs=[vmem, anywhere, anywhere, anywhere],
        out_shape=[
            jax.ShapeDtypeStruct((TOK, 512), F32),
            jax.ShapeDtypeStruct((SIDE, PITCH, COLS), BF),
            jax.ShapeDtypeStruct((3, EDGE, D), BF),
            jax.ShapeDtypeStruct((3, EDGE, D), BF),
        ],
        scratch_shapes=[
            pltpu.VMEM((SIDE * TOK, HIDP), BF),
            pltpu.VMEM((SLOTS, COLS), BF),
            pltpu.VMEM((SIDE, 32, COLS), BF),
            pltpu.VMEM((SIDE * TOK, COLS), BF),
            pltpu.VMEM((SLOTS, NEW_MAX), BF),
            pltpu.VMEM((OLD_MAX, SLOTS), BF),
            pltpu.VMEM((HALF, SIDE * TOK), BF),
            pltpu.VMEM((8, HALF, COLS), F32),
            pltpu.VMEM((8, HALF, COLS), BF),
            pltpu.VMEM((TOK, SLOTS), BF),
            half, half, half, half, half, half, half, half,
            pltpu.VMEM((SIDE, PITCH, COLS), BF),
            pltpu.VMEM((SIDE, TOK, COLS), BF),
            pltpu.VMEM((SIDE, 128, COLS), BF),
            pltpu.VMEM((SIDE, 128, COLS), BF),
            pltpu.VMEM((SIDE, TOK, 512), BF),
            pltpu.VMEM((3, TOK, 512), BF),
            pltpu.SemaphoreType.DMA((80,)),
            pltpu.SemaphoreType.DMA((80,)),
            pltpu.SemaphoreType.DMA((10,)),
        ],
        compiler_params=pltpu.CompilerParams(
            collective_id=0, has_side_effects=True, vmem_limit_bytes=63 * 1024 * 1024
        ),
        name="exchange",
    )(tab, hid, wq, og, pre, suf)


def adam_kernel(scale, tab, master, first, second, left, right, grad, o_m, o_1, o_2, buf):
    me = lax.axis_index("fsdp")
    old_count = tab[1, me]
    count = tab[3, me]
    shift = jnp.clip(tab[2, me] - tab[0, me], -EDGE, CAP + EDGE)
    row = lax.broadcasted_iota(jnp.int32, (CAP, 128), 0)
    live = row < count
    for j in range(master.shape[2] // 128):
        lanes = pl.ds(128 * j, 128)
        moved = []
        for a, ref in enumerate((master, first, second)):
            own = buf.at[3 * j + a]
            own[pl.ds(0, EDGE), :] = left[a, :, lanes].astype(F32)
            own[pl.ds(EDGE, CAP), :] = ref[0, :, lanes]
            own[pl.ds(EDGE + old_count, EDGE), :] = right[a, :, lanes].astype(F32)
            moved.append(own[pl.ds(EDGE + shift, CAP), :])
        weight, one, two = moved
        g = grad[0, pl.ds(0, CAP), lanes].astype(F32) * scale
        one = 0.9 * one + 0.1 * g
        two = 0.95 * two + 0.05 * g * g
        weight = weight - 0.001 * (one / (jnp.sqrt(two) + 1e-08) + 0.1 * weight)
        o_m[0, :, lanes] = jnp.where(live, weight, 0.0)
        o_1[0, :, lanes] = jnp.where(live, one, 0.0)
        o_2[0, :, lanes] = jnp.where(live, two, 0.0)


def adam(tab, master, first, second, left, right, grad, scale):
    wide = 512
    per = COLS // wide
    state = pl.BlockSpec((1, CAP, wide), lambda i: (0, 0, i))
    edge = pl.BlockSpec((3, EDGE, wide), lambda i: (0, 0, i))
    return pl.pallas_call(
        functools.partial(adam_kernel, scale),
        grid=(D // wide,),
        in_specs=[
            pl.BlockSpec(memory_space=pltpu.SMEM),
            state, state, state, edge, edge,
            pl.BlockSpec((1, PITCH, wide), lambda i: (i // per, 0, i % per)),
        ],
        out_specs=[state, state, state],
        out_shape=[jax.ShapeDtypeStruct((1, CAP, D), F32)] * 3,
        scratch_shapes=[pltpu.VMEM((3 * wide // 128, 400, 128), F32)],
        name="adam",
    )(tab, master, first, second, left, right, grad)


def local(gate_act, up_act, out_grad, master_old, moment1_old, moment2_old, old_bounds, new_bounds, rank_map):
    scale = 1.0 / math.sqrt(gate_act.shape[0] * lax.axis_size("fsdp"))
    tab, hid, wq, pre, suf = prep(
        old_bounds, new_bounds, rank_map, gate_act, up_act, master_old, moment1_old, moment2_old
    )
    mlp, grad, left, right = exchange(tab, hid, wq, out_grad, pre, suf)
    master, first, second = adam(
        tab, master_old, moment1_old, moment2_old, left, right, grad, scale
    )
    return mlp, master, first, second


def solution(mesh):
    act = P("fsdp", "dp")
    state = P("dp", "fsdp", None)
    table = P("dp", None)
    return jax.shard_map(
        local,
        mesh=mesh,
        in_specs=(act, act, P("fsdp", None), state, state, state, table, table, table),
        out_specs=(act, state, state, state),
        check_vma=False,
    )
```
